32 devices in a mesh: parts: 2 (over y), len: 4 (over x, core), blk: 4 (over z).
Axes of the slice: x: 2, y: 2, z: 4, core: 2. Of those that a mesh axis runs over, the one named last changes fastest.
Arguments:
- reflection: bfloat16 [8, 2048, 2048], P(('parts', 'len'), None, 'blk'), parts along dimension 0, may hold values from -1 to 1
- transmission: bfloat16 [8, 2048, 2048], P(('parts', 'len'), None, 'blk'), parts along dimension 0, may hold values from -1 to 1
Outputs:
- pair_transmission: float32 [8, 2048, 1024], P(('parts', 'len'), None, 'blk'), parts along dimension 0
The draws below stay inside these ranges and needn't reach their ends.
There are 2 independent parts, one for each index of `parts`. The reference program is written for one: setup_inputs(seed, part) draws one part's arguments, and reference() takes and returns one part's arrays. A program takes and returns all parts, laid end to end along the dimension named above; each array names one. Nothing has to cross between parts.
All inputs are finite; a program needn't handle non-finite values.
Results may differ from the reference program's by a relative error of at most 0.0053.
Values may be sent and summed in bfloat16 or wider, within the bound.
A program may use at most 64 MiB of HBM per device.

```python
import jax
import jax.numpy as jnp
from jax import lax

N = 2048
TERMS = 8
SEGS = 4
N_LEN = 4
N_BLK = 4


def dominant_blocks(key, lo, hi, spread, signed):
    key_diag, key_sign, key_rest = jax.random.split(key, 3)
    eye = jnp.eye(N, dtype=jnp.float32)
    rest = jax.random.normal(key_rest, (SEGS, N, N), jnp.float32) * (spread / N ** 0.5)
    magnitude = jax.random.uniform(key_diag, (SEGS, N), jnp.float32, lo, hi)
    sign = jnp.where(jax.random.bernoulli(key_sign, 0.5, (SEGS, N)), 1.0, -1.0) if signed else jnp.ones((SEGS, N), jnp.float32)
    diagonal = (magnitude * sign)[:, :, None] * eye[None]
    whole = rest * (1.0 - eye)[None] + diagonal
    return jnp.clip(whole, -1.0, 1.0).astype(jnp.bfloat16)


def draw_reflection(key, part):
    return dominant_blocks(jax.random.fold_in(key, 11), 0.5, 0.85, 0.2, True)


def draw_transmission(key, part):
    return dominant_blocks(jax.random.fold_in(key, 23), 0.4, 0.8, 0.3, False)


def setup_inputs(seed: int = 0, part: int = 0) -> dict:
    keys = jax.random.split(jax.random.key(seed), 3)
    part_keys = jax.random.split(jax.random.fold_in(keys[2], part), 3)
    reflection = draw_reflection(jax.random.fold_in(jax.random.fold_in(keys[2], part), 71), part)
    transmission = draw_transmission(jax.random.fold_in(jax.random.fold_in(keys[2], part), 71), part)
    return dict(reflection=reflection, transmission=transmission)


def reference(reflection, transmission):
    width = N // (2 * N_BLK)
    highest = lax.Precision.HIGHEST
    results = []
    for pair in range(N_LEN // 2):
        inner_right = reflection[2 * pair].astype(jnp.float32)
        inner_left = reflection[2 * pair + 1].astype(jnp.float32)
        first = transmission[2 * pair]
        second = transmission[2 * pair + 1].astype(jnp.float32)
        coupling = jnp.dot(inner_right, inner_left, precision=highest).astype(jnp.bfloat16)
        coupling_wide = coupling.astype(jnp.float32)
        first_wide = first.astype(jnp.float32)
        state = first
        for term in range(TERMS - 1):
            state = (first_wide + jnp.dot(coupling_wide, state.astype(jnp.float32), precision=highest)).astype(jnp.bfloat16)
        combined = jnp.dot(second, state.astype(jnp.float32), precision=highest)
        grid = combined.reshape(N, N_BLK, 2, width)
        results.append(grid[:, :, 0, :].reshape(N, N // 2))
        results.append(grid[:, :, 1, :].reshape(N, N // 2))
    return jnp.stack(results)
```

```python
import functools

import jax
import jax.numpy as jnp
from jax import lax
from jax.experimental import pallas as pl
from jax.experimental.pallas import tpu as pltpu
from jax.sharding import PartitionSpec as P

TERMS = 8
CHUNKS = 8
MESH = pl.DeviceIdType.MESH
L, R, S = 0, 1, 2


def from_partner(block, axis, apart):
    count = lax.axis_size(axis)
    route = []
    for low in range(count):
        high = low | 1 << apart
        if high != low and high < count:
            route += [(low, high), (high, low)]
    return lax.ppermute(block, axis, route)


def on_device(reflection, transmission):
    refl = reflection[0]
    trans = transmission[0]
    panel = refl.shape[1]
    width = panel // 2
    parity = lax.axis_index("len") % 2
    is_odd = parity == 1
    other_refl, other_trans = from_partner((refl, trans), "len", 0)
    inner_right = jnp.where(is_odd, other_refl, refl)
    inner_left = jnp.where(is_odd, refl, other_refl)
    first = jnp.where(is_odd, other_trans, trans)
    second = jnp.where(is_odd, trans, other_trans)
    rows = inner_left
    coupling_cols = jnp.dot(
        lax.all_gather(inner_right, "blk", axis=1, tiled=True),
        rows,
        preferred_element_type=jnp.float32,
    ).astype(jnp.bfloat16)
    piece = lax.all_gather(coupling_cols, "blk", axis=1, tiled=True)
    rows = first
    product = jnp.dot(piece, rows, preferred_element_type=jnp.float32)
    first_wide = first.astype(jnp.float32)
    state = (first_wide + product).astype(jnp.bfloat16)
    for term in range(TERMS - 2):
        state = (first_wide + jnp.dot(piece, state, preferred_element_type=jnp.float32)).astype(
            jnp.bfloat16
        )
    rows = state
    combined = jnp.dot(
        lax.all_gather(second, "blk", axis=1, tiled=True), rows, preferred_element_type=jnp.float32
    )
    combined = lax.dynamic_slice_in_dim(combined, parity * width, width, 1)
    return combined[None]


def loop(count, body, start=0):
    def step(i, carry):
        body(i)
        return carry

    lax.fori_loop(start, count, step, 0)


def line_kernel(
    n, refl, trans, out, x, coupling, first, state, far_in, far_out,
    got, sent, first_got, first_sent, far_got, far_sent,
):
    size, panel = refl.shape[1:]
    width = panel // 2
    chunk = size // CHUNKS
    low, high = n // 2 - 1, n // 2
    z, along = lax.axis_index("blk"), lax.axis_index("len")
    half = lax.rem(along, 2)
    odd, even = half == 1, half == 0
    mate = along + 1 - 2 * half
    lower = z <= low
    mid = jnp.where(lower, low, high)
    end = jnp.where(lower, low - 1, high + 1)
    other_mid = jnp.where(lower, high, low)
    other_end = jnp.where(lower, high + 1, low - 1)
    inner = z == mid
    outer = z == end

    barrier = pltpu.get_barrier_semaphore()

    def greet(**place):
        pl.semaphore_signal(barrier, inc=1, device_id=place, device_id_type=MESH)

    greet(len=mate)

    @pl.when(inner)
    def _():
        for there in (end, other_mid):
            greet(blk=there)
        greet(blk=end, len=mate)
        pl.semaphore_wait(barrier, 4)

    @pl.when(outer)
    def _():
        greet(blk=mid)
        greet(blk=mid, len=mate)
        pl.semaphore_wait(barrier, 3)

    def rows(i):
        return pl.ds(pl.multiple_of(i * chunk, chunk), chunk)

    def place(m, block, i):
        return x.at[m, rows(i), pl.ds(pl.multiple_of(block * panel, panel), panel)]

    def own(m, i):
        return (trans if m == S else refl).at[0, rows(i), :]

    def local(m, i):
        return pltpu.make_async_copy(own(m, i), place(m, z, i), got.at[m, z, i])

    def wait(m, block, i):
        here = place(m, block, i)
        pltpu.make_async_copy(here, here, got.at[m, block, i]).wait()

    def send(m, block, i, way, mine=False):
        where = ({"blk": other_mid}, {"len": mate}, {"blk": mid})[way]
        return pltpu.make_async_remote_copy(
            src_ref=own(m, i) if mine else place(m, block, i),
            dst_ref=place(m, block, i),
            send_sem=sent.at[m, block, i, min(way, 1)],
            recv_sem=got.at[m, block, i],
            device_id=where,
            device_id_type=MESH,
        )

    def first_copy(side, slot, sem, where):
        return pltpu.make_async_remote_copy(
            src_ref=trans.at[0, :, side],
            dst_ref=first.at[slot],
            send_sem=first_sent.at[sem],
            recv_sem=first_got.at[slot],
            device_id=where,
            device_id_type=MESH,
        )

    def far(i):
        return pltpu.make_async_remote_copy(
            src_ref=far_out.at[rows(i), :],
            dst_ref=far_in.at[rows(i), :],
            send_sem=far_sent.at[i],
            recv_sem=far_got.at[i],
            device_id={"blk": end},
            device_id_type=MESH,
        )

    near_side, far_side = pl.ds(0, width), pl.ds(width, width)
    near_first = first_copy(near_side, 0, 0, {"blk": mid})
    cross_first = first_copy(far_side, 0, 1, {"blk": mid, "len": mate})
    mate_first = first_copy(far_side, 1, 0, {"len": mate})
    own_first = pltpu.make_async_copy(trans.at[0, :, near_side], first.at[1], first_got.at[1])

    def first_wait(slot):
        pltpu.make_async_copy(first.at[slot], first.at[slot], first_got.at[slot]).wait()

    @pl.when(outer & even)
    def _():
        loop(CHUNKS, lambda i: send(R, z, i, 2, True).start())
        near_first.start()
        cross_first.start()

    @pl.when(outer & odd)
    def _():
        loop(CHUNKS, lambda i: send(L, z, i, 2, True).start())
        loop(CHUNKS, lambda i: send(S, z, i, 2, True).start())

    @pl.when(outer)
    def _():
        def back(i):
            far(i).wait_recv()
            out[0, rows(i), :] = far_in[rows(i), :].astype(jnp.float32)

        loop(CHUNKS, back)

    @pl.when(outer & even)
    def _():
        loop(CHUNKS, lambda i: send(R, z, i, 2, True).wait_send())
        near_first.wait_send()
        cross_first.wait_send()

    @pl.when(outer & odd)
    def _():
        loop(CHUNKS, lambda i: send(L, z, i, 2, True).wait_send())
        loop(CHUNKS, lambda i: send(S, z, i, 2, True).wait_send())

    tile = size // 4

    def couple(i):
        def columns(t):
            c = pl.ds(pl.multiple_of(t * tile, tile), tile)
            coupling[rows(i), c] = jnp.dot(
                x[R, rows(i), :], x[L, :, c], preferred_element_type=jnp.float32
            ).astype(jnp.bfloat16)

        loop(4, columns)

    def pass_on(m, block, i):
        wait(m, block, i)
        send(m, block, i, 1).start()

    @pl.when(inner & even)
    def _():
        def begin(i):
            local(R, i).start()
            send(R, z, i, 1, True).start()

        loop(CHUNKS, begin)
        own_first.start()
        mate_first.start()
        loop(CHUNKS, lambda i: pass_on(R, end, i))
        for block in (z, end, other_mid):
            loop(CHUNKS, lambda i, block=block: wait(L, block, i))
        loop(CHUNKS - 1, lambda i: wait(L, other_end, i))

        def across(i):
            send(R, z, i, 0, True).start()
            send(R, end, i, 0).start()

        loop(CHUNKS, across)
        wait(L, other_end, CHUNKS - 1)

        def work(i):
            wait(R, z, i)
            pass_on(R, other_mid, i)
            pass_on(R, other_end, i)
            couple(i)

        loop(CHUNKS, work)

    @pl.when(inner & odd)
    def _():
        def begin(i):
            send(L, z, i, 0, True).start()
            send(L, z, i, 1, True).start()
            local(L, i).start()

        loop(CHUNKS, begin)
        loop(CHUNKS, lambda i: local(S, i).start())

        def both(i):
            wait(L, end, i)
            send(L, end, i, 0).start()
            send(L, end, i, 1).start()

        loop(CHUNKS, both)
        loop(CHUNKS, lambda i: pass_on(L, other_mid, i))
        loop(CHUNKS, lambda i: pass_on(L, other_end, i))
        loop(CHUNKS, lambda i: send(S, z, i, 1, True).start())
        loop(CHUNKS, lambda i: wait(L, z, i))

        def across(i):
            wait(S, end, i)
            send(S, z, i, 0, True).start()
            send(S, end, i, 0).start()
            send(S, end, i, 1).start()

        def work(i):
            for block in range(n):
                wait(R, block, i)

            @pl.when(i == CHUNKS - 2)
            def _():
                loop(CHUNKS // 2, across)

            couple(i)

        loop(CHUNKS, work)
        loop(CHUNKS, across, CHUNKS // 2)

    @pl.when(inner)
    def _():
        steps = TERMS - 1
        first_wait(0)
        first_wait(1)
        state[:, 0] = first[...]

        def advance(slot, before, after):
            def part(t):
                r = pl.ds(pl.multiple_of(t * tile, tile), tile)
                product = jnp.dot(coupling[r, :], state[slot, before], preferred_element_type=jnp.float32)
                state[slot, after, r, :] = (first[slot, r, :].astype(jnp.float32) + product).astype(jnp.bfloat16)

            loop(4, part)

        def arrived(i):
            wait(S, z, i)

            @pl.when(even)
            def _():
                for block in (end, other_mid, other_end):
                    wait(S, block, i)

        def far_product(i):
            arrived(i)
            far_out[rows(i), :] = jnp.dot(
                x[S, rows(i), :], state[0, steps % 2], preferred_element_type=jnp.float32
            ).astype(jnp.bfloat16)
            far(i).start()

        def near_product(i):
            out[0, rows(i), :] = jnp.dot(
                x[S, rows(i), :], state[1, steps % 2], preferred_element_type=jnp.float32
            )

        def relay(i):
            @pl.when(odd)
            def _():
                pass_on(S, other_mid, i)
                pass_on(S, other_end, i)

        for slot in range(2):
            def turn(k, slot=slot):
                advance(slot, lax.rem(k, 2), lax.rem(k + 1, 2))
                g = k + slot * steps
                @pl.when(lax.rem(g, 2) == 1)
                def _():
                    relay((g - 1) // 2)
                if slot == 1:
                    @pl.when(lax.rem(g, 2) == 0)
                    def _():
                        far_product(g // 2 - 1)

            loop(steps, turn)
            if slot == 0:
                loop(steps // 2, far_product)
        far_product(CHUNKS - 2)
        loop(CHUNKS - 1, near_product)
        relay(CHUNKS - 1)
        far_product(CHUNKS - 1)
        near_product(CHUNKS - 1)
        loop(CHUNKS, lambda i: far(i).wait_send())

    @pl.when(inner & even)
    def _():
        mate_first.wait_send()

        def drain(i):
            for way in range(2):
                send(R, z, i, way, True).wait_send()
                send(R, end, i, way).wait_send()
            send(R, other_mid, i, 1).wait_send()
            send(R, other_end, i, 1).wait_send()

        loop(CHUNKS, drain)

    @pl.when(inner & odd)
    def _():
        def drain(i):
            for m in (L, S):
                for way in range(2):
                    send(m, z, i, way, True).wait_send()
                    send(m, end, i, way).wait_send()
                send(m, other_mid, i, 1).wait_send()
                send(m, other_end, i, 1).wait_send()

        loop(CHUNKS, drain)


def line(n, reflection, transmission):
    size, panel = reflection.shape[1:]
    width = panel // 2
    bf16 = jnp.bfloat16
    return pl.pallas_call(
        functools.partial(line_kernel, n),
        out_shape=jax.ShapeDtypeStruct((1, size, width), jnp.float32),
        in_specs=[pl.BlockSpec(memory_space=pl.ANY)] * 2,
        out_specs=pl.BlockSpec(memory_space=pltpu.VMEM),
        scratch_shapes=[
            pltpu.VMEM((3, size, n * panel), bf16),
            pltpu.VMEM((size, n * panel), bf16),
            pltpu.VMEM((2, size, width), bf16),
            pltpu.VMEM((2, 2, size, width), bf16),
            pltpu.VMEM((size, width), bf16),
            pltpu.VMEM((size, width), bf16),
            pltpu.SemaphoreType.DMA((3, n, CHUNKS)),
            pltpu.SemaphoreType.DMA((3, n, CHUNKS, 2)),
            pltpu.SemaphoreType.DMA((2,)),
            pltpu.SemaphoreType.DMA((2,)),
            pltpu.SemaphoreType.DMA((CHUNKS,)),
            pltpu.SemaphoreType.DMA((CHUNKS,)),
        ],
        compiler_params=pltpu.CompilerParams(
            collective_id=0, has_side_effects=True, vmem_limit_bytes=60 * 2**20
        ),
    )(reflection, transmission)


def solution(mesh):
    n = mesh.shape["blk"]
    return jax.shard_map(
        functools.partial(line, n) if n == 4 else on_device,
        mesh=mesh,
        in_specs=(P(("parts", "len"), None, "blk"), P(("parts", "len"), None, "blk")),
        out_specs=P(("parts", "len"), None, "blk"),
        check_vma=False,
    )
```

```python
import functools

import jax
import jax.numpy as jnp
from jax import lax
from jax.experimental import pallas as pl
from jax.experimental.pallas import tpu as pltpu
from jax.sharding import PartitionSpec as P

TERMS = 8
CHUNKS = 8
LATE = 5
MESH = pl.DeviceIdType.MESH
L, R, S = 0, 1, 2


def from_partner(block, axis, apart):
    count = lax.axis_size(axis)
    route = []
    for low in range(count):
        high = low | 1 << apart
        if high != low and high < count:
            route += [(low, high), (high, low)]
    return lax.ppermute(block, axis, route)


def on_device(reflection, transmission):
    refl = reflection[0]
    trans = transmission[0]
    panel = refl.shape[1]
    width = panel // 2
    parity = lax.axis_index("len") % 2
    is_odd = parity == 1
    other_refl, other_trans = from_partner((refl, trans), "len", 0)
    inner_right = jnp.where(is_odd, other_refl, refl)
    inner_left = jnp.where(is_odd, refl, other_refl)
    first = jnp.where(is_odd, other_trans, trans)
    second = jnp.where(is_odd, trans, other_trans)
    rows = inner_left
    coupling_cols = jnp.dot(
        lax.all_gather(inner_right, "blk", axis=1, tiled=True),
        rows,
        preferred_element_type=jnp.float32,
    ).astype(jnp.bfloat16)
    piece = lax.all_gather(coupling_cols, "blk", axis=1, tiled=True)
    rows = first
    product = jnp.dot(piece, rows, preferred_element_type=jnp.float32)
    first_wide = first.astype(jnp.float32)
    state = (first_wide + product).astype(jnp.bfloat16)
    for term in range(TERMS - 2):
        state = (first_wide + jnp.dot(piece, state, preferred_element_type=jnp.float32)).astype(
            jnp.bfloat16
        )
    rows = state
    combined = jnp.dot(
        lax.all_gather(second, "blk", axis=1, tiled=True), rows, preferred_element_type=jnp.float32
    )
    combined = lax.dynamic_slice_in_dim(combined, parity * width, width, 1)
    return combined[None]


def loop(count, body, start=0):
    def step(i, carry):
        body(i)
        return carry

    lax.fori_loop(start, count, step, 0)


def line_kernel(
    n, refl, trans, out, x, coupling, first, state, far_in, far_out,
    got, sent, first_got, first_sent, far_got, far_sent, turn_over,
):
    size, panel = refl.shape[1:]
    width = panel // 2
    chunk = size // CHUNKS
    low, high = n // 2 - 1, n // 2
    z, along = lax.axis_index("blk"), lax.axis_index("len")
    half = lax.rem(along, 2)
    odd, even = half == 1, half == 0
    mate = along + 1 - 2 * half
    lower = z <= low
    mid = jnp.where(lower, low, high)
    end = jnp.where(lower, low - 1, high + 1)
    other_mid = jnp.where(lower, high, low)
    other_end = jnp.where(lower, high + 1, low - 1)
    inner = z == mid
    outer = z == end

    barrier = pltpu.get_barrier_semaphore()

    def greet(**place):
        pl.semaphore_signal(barrier, inc=1, device_id=place, device_id_type=MESH)

    greet(len=mate)

    @pl.when(inner)
    def _():
        for there in (end, other_mid):
            greet(blk=there)
            greet(blk=there, len=mate)
        pl.semaphore_wait(barrier, 5)

    @pl.when(outer)
    def _():
        greet(blk=mid)
        greet(blk=mid, len=mate)
        pl.semaphore_wait(barrier, 3)

    def rows(i):
        return pl.ds(pl.multiple_of(i * chunk, chunk), chunk)

    def place(m, block, i):
        return x.at[m, rows(i), pl.ds(pl.multiple_of(block * panel, panel), panel)]

    def own(m, i):
        return (trans if m == S else refl).at[0, rows(i), :]

    def local(m, i):
        return pltpu.make_async_copy(own(m, i), place(m, z, i), got.at[m, z, i])

    def wait(m, block, i):
        here = place(m, block, i)
        pltpu.make_async_copy(here, here, got.at[m, block, i]).wait()

    def send(m, block, i, way, mine=False):
        where = ({"blk": other_mid, "len": mate}, {"len": mate}, {"blk": mid})[way]
        return pltpu.make_async_remote_copy(
            src_ref=own(m, i) if mine else place(m, block, i),
            dst_ref=place(m, block, i),
            send_sem=sent.at[m, block, i, min(way, 1)],
            recv_sem=got.at[m, block, i],
            device_id=where,
            device_id_type=MESH,
        )

    def first_copy(side, slot, sem, where):
        return pltpu.make_async_remote_copy(
            src_ref=trans.at[0, :, side],
            dst_ref=first.at[slot],
            send_sem=first_sent.at[sem],
            recv_sem=first_got.at[slot],
            device_id=where,
            device_id_type=MESH,
        )

    def far(i):
        return pltpu.make_async_remote_copy(
            src_ref=far_out.at[rows(i), :],
            dst_ref=far_in.at[rows(i), :],
            send_sem=far_sent.at[i],
            recv_sem=far_got.at[i],
            device_id={"blk": end},
            device_id_type=MESH,
        )

    near_side, far_side = pl.ds(0, width), pl.ds(width, width)
    near_first = first_copy(near_side, 0, 0, {"blk": mid})
    cross_first = first_copy(far_side, 0, 1, {"blk": mid, "len": mate})
    mate_first = first_copy(far_side, 1, 0, {"len": mate})
    own_first = pltpu.make_async_copy(trans.at[0, :, near_side], first.at[1], first_got.at[1])

    def first_wait(slot):
        pltpu.make_async_copy(first.at[slot], first.at[slot], first_got.at[slot]).wait()

    @pl.when(outer & even)
    def _():
        loop(CHUNKS, lambda i: send(R, z, i, 2, True).start())
        near_first.start()
        cross_first.start()
        near_first.wait_send()
        pl.semaphore_signal(turn_over, inc=1, device_id={"len": mate}, device_id_type=MESH)

    @pl.when(outer & odd)
    def _():
        loop(CHUNKS, lambda i: send(L, z, i, 2, True).start())
        pl.semaphore_wait(turn_over, 1)
        loop(CHUNKS, lambda i: send(S, z, i, 2, True).start())

    @pl.when(outer)
    def _():
        def back(i):
            far(i).wait_recv()
            out[0, rows(i), :] = far_in[rows(i), :].astype(jnp.float32)

        loop(CHUNKS, back)

    @pl.when(outer & even)
    def _():
        loop(CHUNKS, lambda i: send(R, z, i, 2, True).wait_send())
        cross_first.wait_send()

    @pl.when(outer & odd)
    def _():
        loop(CHUNKS, lambda i: send(L, z, i, 2, True).wait_send())
        loop(CHUNKS, lambda i: send(S, z, i, 2, True).wait_send())

    tile = size // 4

    def couple(i):
        def columns(t):
            c = pl.ds(pl.multiple_of(t * tile, tile), tile)
            coupling[rows(i), c] = jnp.dot(
                x[R, rows(i), :], x[L, :, c], preferred_element_type=jnp.float32
            ).astype(jnp.bfloat16)

        loop(4, columns)

    def begin_state(slot, i):
        product = jnp.dot(coupling[rows(i), :], first[slot], preferred_element_type=jnp.float32)
        state[slot, 1, rows(i), :] = (
            first[slot, rows(i), :].astype(jnp.float32) + product
        ).astype(jnp.bfloat16)

    def couple_and_begin(i):
        couple(i)
        begin_state(1, i)

        @pl.when(i == LATE)
        def _():
            first_wait(0)
            loop(LATE, lambda k: begin_state(0, k))

        @pl.when(i >= LATE)
        def _():
            begin_state(0, i)

    def pass_on(m, block, i):
        wait(m, block, i)
        send(m, block, i, 1).start()

    @pl.when(inner & even)
    def _():
        def begin(i):
            local(R, i).start()
            send(R, z, i, 1, True).start()

        loop(CHUNKS, begin)
        own_first.start()
        mate_first.start()
        loop(CHUNKS, lambda i: pass_on(R, end, i))
        loop(CHUNKS, lambda i: pass_on(L, other_mid, i))
        loop(CHUNKS - 1, lambda i: pass_on(L, other_end, i))

        def across(i):
            send(R, z, i, 0, True).start()
            send(R, end, i, 0).start()

        loop(CHUNKS, across)
        pass_on(L, other_end, CHUNKS - 1)
        for block in (z, end):
            loop(CHUNKS, lambda i, block=block: wait(L, block, i))

        first_wait(1)

        def work(i):
            for block in (z, other_mid, other_end):
                wait(R, block, i)
            couple_and_begin(i)

        loop(CHUNKS, work)

    @pl.when(inner & odd)
    def _():
        def begin(i):
            send(L, z, i, 0, True).start()
            send(L, z, i, 1, True).start()
            local(L, i).start()

        loop(CHUNKS, begin)
        loop(CHUNKS, lambda i: local(S, i).start())

        def both(i):
            pass_on(L, end, i)
            send(L, end, i, 0).start()

        loop(CHUNKS, both)
        loop(CHUNKS, lambda i: send(S, z, i, 1, True).start())
        for block in (z, other_mid, other_end):
            loop(CHUNKS, lambda i, block=block: wait(L, block, i))

        def across(i):
            pass_on(S, end, i)
            send(S, z, i, 0, True).start()
            send(S, end, i, 0).start()

        first_wait(1)

        def work(i):
            pass_on(R, other_mid, i)
            pass_on(R, other_end, i)
            for block in (z, end):
                wait(R, block, i)

            @pl.when(i == CHUNKS - 2)
            def _():
                loop(CHUNKS // 2, across)

            couple_and_begin(i)

        loop(CHUNKS, work)
        loop(CHUNKS, across, CHUNKS // 2)

    @pl.when(inner)
    def _():
        steps = TERMS - 1
        def advance(slot, before, after):
            tall = size // 1

            def part(t):
                r = pl.ds(pl.multiple_of(t * tall, tall), tall)
                product = jnp.dot(coupling[r, :], state[slot, before], preferred_element_type=jnp.float32)
                state[slot, after, r, :] = (first[slot, r, :].astype(jnp.float32) + product).astype(jnp.bfloat16)

            loop(1, part)

        def arrived(i):
            wait(S, z, i)

            @pl.when(even)
            def _():
                wait(S, end, i)

            @pl.when(odd)
            def _():
                for block in (other_mid, other_end):
                    wait(S, block, i)

        def far_product(i):
            arrived(i)
            far_out[rows(i), :] = jnp.dot(
                x[S, rows(i), :], state[0, steps % 2], preferred_element_type=jnp.float32
            ).astype(jnp.bfloat16)
            far(i).start()

        def near_product(i):
            out[0, rows(i), :] = jnp.dot(
                x[S, rows(i), :], state[1, steps % 2], preferred_element_type=jnp.float32
            )

        def relay(i):
            @pl.when(even)
            def _():
                pass_on(S, other_mid, i)
                pass_on(S, other_end, i)

        turns = steps - 1

        def early(k):
            advance(0, lax.rem(k, 2), lax.rem(k + 1, 2))

            @pl.when(lax.rem(k, 2) == 0)
            def _():
                relay(k // 2 - 1)

        def late(k):
            advance(1, lax.rem(k, 2), lax.rem(k + 1, 2))

            @pl.when(lax.rem(k, 2) == 0)
            def _():
                relay(k // 2 - 1 + turns // 2)
                far_product(k // 2 - 1 + turns // 2)

        loop(steps, early, 1)
        loop(turns // 2, far_product)
        loop(steps, late, 1)
        relay(CHUNKS - 2)
        far_product(CHUNKS - 2)
        loop(CHUNKS - 1, near_product)
        relay(CHUNKS - 1)
        far_product(CHUNKS - 1)
        near_product(CHUNKS - 1)
        loop(CHUNKS, lambda i: far(i).wait_send())

    def drain_own(m, i):
        for way in range(2):
            send(m, z, i, way, True).wait_send()
            send(m, end, i, way).wait_send()

    def drain_relay(m, i):
        send(m, other_mid, i, 1).wait_send()
        send(m, other_end, i, 1).wait_send()

    @pl.when(inner & even)
    def _():
        mate_first.wait_send()

        def drain(i):
            drain_own(R, i)
            drain_relay(L, i)
            drain_relay(S, i)

        loop(CHUNKS, drain)

    @pl.when(inner & odd)
    def _():
        def drain(i):
            drain_own(L, i)
            drain_own(S, i)
            drain_relay(R, i)

        loop(CHUNKS, drain)


def line(n, reflection, transmission):
    size, panel = reflection.shape[1:]
    width = panel // 2
    bf16 = jnp.bfloat16
    return pl.pallas_call(
        functools.partial(line_kernel, n),
        out_shape=jax.ShapeDtypeStruct((1, size, width), jnp.float32),
        in_specs=[pl.BlockSpec(memory_space=pl.ANY)] * 2,
        out_specs=pl.BlockSpec(memory_space=pltpu.VMEM),
        scratch_shapes=[
            pltpu.VMEM((3, size, n * panel), bf16),
            pltpu.VMEM((size, n * panel), bf16),
            pltpu.VMEM((2, size, width), bf16),
            pltpu.VMEM((2, 2, size, width), bf16),
            pltpu.VMEM((size, width), bf16),
            pltpu.VMEM((size, width), bf16),
            pltpu.SemaphoreType.DMA((3, n, CHUNKS)),
            pltpu.SemaphoreType.DMA((3, n, CHUNKS, 2)),
            pltpu.SemaphoreType.DMA((2,)),
            pltpu.SemaphoreType.DMA((2,)),
            pltpu.SemaphoreType.DMA((CHUNKS,)),
            pltpu.SemaphoreType.DMA((CHUNKS,)),
            pltpu.SemaphoreType.REGULAR,
        ],
        compiler_params=pltpu.CompilerParams(
            collective_id=0, has_side_effects=True, vmem_limit_bytes=60 * 2**20
        ),
    )(reflection, transmission)


def solution(mesh):
    n = mesh.shape["blk"]
    return jax.shard_map(
        functools.partial(line, n) if n == 4 else on_device,
        mesh=mesh,
        in_specs=(P(("parts", "len"), None, "blk"), P(("parts", "len"), None, "blk")),
        out_specs=P(("parts", "len"), None, "blk"),
        check_vma=False,
    )
```

```python
import functools

import jax
import jax.numpy as jnp
from jax import lax
from jax.experimental import pallas as pl
from jax.experimental.pallas import tpu as pltpu
from jax.sharding import PartitionSpec as P

TERMS = 8
CHUNKS = 8
LATE = 5
MESH = pl.DeviceIdType.MESH
L, R, S = 0, 1, 2


def from_partner(block, axis, apart):
    count = lax.axis_size(axis)
    route = []
    for low in range(count):
        high = low | 1 << apart
        if high != low and high < count:
            route += [(low, high), (high, low)]
    return lax.ppermute(block, axis, route)


def on_device(reflection, transmission):
    refl = reflection[0]
    trans = transmission[0]
    panel = refl.shape[1]
    width = panel // 2
    parity = lax.axis_index("len") % 2
    is_odd = parity == 1
    other_refl, other_trans = from_partner((refl, trans), "len", 0)
    inner_right = jnp.where(is_odd, other_refl, refl)
    inner_left = jnp.where(is_odd, refl, other_refl)
    first = jnp.where(is_odd, other_trans, trans)
    second = jnp.where(is_odd, trans, other_trans)
    rows = inner_left
    coupling_cols = jnp.dot(
        lax.all_gather(inner_right, "blk", axis=1, tiled=True),
        rows,
        preferred_element_type=jnp.float32,
    ).astype(jnp.bfloat16)
    piece = lax.all_gather(coupling_cols, "blk", axis=1, tiled=True)
    rows = first
    product = jnp.dot(piece, rows, preferred_element_type=jnp.float32)
    first_wide = first.astype(jnp.float32)
    state = (first_wide + product).astype(jnp.bfloat16)
    for term in range(TERMS - 2):
        state = (first_wide + jnp.dot(piece, state, preferred_element_type=jnp.float32)).astype(
            jnp.bfloat16
        )
    rows = state
    combined = jnp.dot(
        lax.all_gather(second, "blk", axis=1, tiled=True), rows, preferred_element_type=jnp.float32
    )
    combined = lax.dynamic_slice_in_dim(combined, parity * width, width, 1)
    return combined[None]


def loop(count, body, start=0):
    def step(i, carry):
        body(i)
        return carry

    lax.fori_loop(start, count, step, 0)


def line_kernel(
    n, refl, trans, out, x, coupling, first, state, far_in, far_out,
    got, sent, first_got, first_sent, far_got, far_sent, turn_over, result, written,
):
    size, panel = refl.shape[1:]
    width = panel // 2
    chunk = size // CHUNKS
    low, high = n // 2 - 1, n // 2
    z, along = lax.axis_index("blk"), lax.axis_index("len")
    half = lax.rem(along, 2)
    odd, even = half == 1, half == 0
    mate = along + 1 - 2 * half
    lower = z <= low
    mid = jnp.where(lower, low, high)
    end = jnp.where(lower, low - 1, high + 1)
    other_mid = jnp.where(lower, high, low)
    other_end = jnp.where(lower, high + 1, low - 1)
    inner = z == mid
    outer = z == end

    barrier = pltpu.get_barrier_semaphore()

    def greet(**place):
        pl.semaphore_signal(barrier, inc=1, device_id=place, device_id_type=MESH)

    greet(len=mate)

    @pl.when(inner)
    def _():
        for there in (end, other_mid):
            greet(blk=there)
            greet(blk=there, len=mate)
        pl.semaphore_wait(barrier, 5)

    @pl.when(outer)
    def _():
        greet(blk=mid)
        greet(blk=mid, len=mate)
        pl.semaphore_wait(barrier, 3)

    def rows(i):
        return pl.ds(pl.multiple_of(i * chunk, chunk), chunk)

    def place(m, block, i):
        return x.at[m, rows(i), pl.ds(pl.multiple_of(block * panel, panel), panel)]

    def own(m, i):
        return (trans if m == S else refl).at[0, rows(i), :]

    def local(m, i):
        return pltpu.make_async_copy(own(m, i), place(m, z, i), got.at[m, z, i])

    def wait(m, block, i):
        here = place(m, block, i)
        pltpu.make_async_copy(here, here, got.at[m, block, i]).wait()

    def send(m, block, i, way, mine=False):
        where = ({"blk": other_mid, "len": mate}, {"len": mate}, {"blk": mid})[way]
        return pltpu.make_async_remote_copy(
            src_ref=own(m, i) if mine else place(m, block, i),
            dst_ref=place(m, block, i),
            send_sem=sent.at[m, block, i, min(way, 1)],
            recv_sem=got.at[m, block, i],
            device_id=where,
            device_id_type=MESH,
        )

    def first_copy(side, slot, sem, where):
        return pltpu.make_async_remote_copy(
            src_ref=trans.at[0, :, side],
            dst_ref=first.at[slot],
            send_sem=first_sent.at[sem],
            recv_sem=first_got.at[slot],
            device_id=where,
            device_id_type=MESH,
        )

    def far(i):
        return pltpu.make_async_remote_copy(
            src_ref=far_out.at[rows(i), :],
            dst_ref=far_in.at[rows(i), :],
            send_sem=far_sent.at[i],
            recv_sem=far_got.at[i],
            device_id={"blk": end},
            device_id_type=MESH,
        )

    def write(i):
        return pltpu.make_async_copy(result.at[rows(i), :], out.at[0, rows(i), :], written.at[i])

    near_side, far_side = pl.ds(0, width), pl.ds(width, width)
    near_first = first_copy(near_side, 0, 0, {"blk": mid})
    cross_first = first_copy(far_side, 0, 1, {"blk": mid, "len": mate})
    mate_first = first_copy(far_side, 1, 0, {"len": mate})
    own_first = pltpu.make_async_copy(trans.at[0, :, near_side], first.at[1], first_got.at[1])

    def first_wait(slot):
        pltpu.make_async_copy(first.at[slot], first.at[slot], first_got.at[slot]).wait()

    @pl.when(outer & even)
    def _():
        loop(CHUNKS, lambda i: send(R, z, i, 2, True).start())
        near_first.start()
        cross_first.start()
        near_first.wait_send()
        pl.semaphore_signal(turn_over, inc=1, device_id={"len": mate}, device_id_type=MESH)

    @pl.when(outer & odd)
    def _():
        loop(CHUNKS, lambda i: send(L, z, i, 2, True).start())
        pl.semaphore_wait(turn_over, 1)
        loop(CHUNKS, lambda i: send(S, z, i, 2, True).start())

    @pl.when(outer)
    def _():
        def back(i):
            far(i).wait_recv()
            result[rows(i), :] = far_in[rows(i), :].astype(jnp.float32)
            write(i).start()

        loop(CHUNKS, back)
        loop(CHUNKS, lambda i: write(i).wait())

    @pl.when(outer & even)
    def _():
        loop(CHUNKS, lambda i: send(R, z, i, 2, True).wait_send())
        cross_first.wait_send()

    @pl.when(outer & odd)
    def _():
        loop(CHUNKS, lambda i: send(L, z, i, 2, True).wait_send())
        loop(CHUNKS, lambda i: send(S, z, i, 2, True).wait_send())

    tile = size // 4

    def couple(i):
        def columns(t):
            c = pl.ds(pl.multiple_of(t * tile, tile), tile)
            coupling[rows(i), c] = jnp.dot(
                x[R, rows(i), :], x[L, :, c], preferred_element_type=jnp.float32
            ).astype(jnp.bfloat16)

        loop(4, columns)

    def begin_state(slot, i):
        product = jnp.dot(coupling[rows(i), :], first[slot], preferred_element_type=jnp.float32)
        state[slot, 1, rows(i), :] = (
            first[slot, rows(i), :].astype(jnp.float32) + product
        ).astype(jnp.bfloat16)

    def couple_and_begin(i):
        couple(i)
        begin_state(1, i)

        @pl.when(i == LATE)
        def _():
            first_wait(0)
            loop(LATE, lambda k: begin_state(0, k))

        @pl.when(i >= LATE)
        def _():
            begin_state(0, i)

    def pass_on(m, block, i):
        wait(m, block, i)
        send(m, block, i, 1).start()

    @pl.when(inner & even)
    def _():
        def begin(i):
            local(R, i).start()
            send(R, z, i, 1, True).start()

        loop(CHUNKS, begin)
        own_first.start()
        mate_first.start()
        loop(CHUNKS, lambda i: pass_on(R, end, i))
        loop(CHUNKS, lambda i: pass_on(L, other_mid, i))
        loop(CHUNKS // 2, lambda i: pass_on(L, other_end, i))

        def across(i):
            send(R, z, i, 0, True).start()
            send(R, end, i, 0).start()

        loop(CHUNKS, across)
        loop(CHUNKS, lambda i: pass_on(L, other_end, i), CHUNKS // 2)
        for block in (z, end):
            loop(CHUNKS, lambda i, block=block: wait(L, block, i))

        first_wait(1)

        def work(i):
            for block in (z, other_mid, other_end):
                wait(R, block, i)
            couple_and_begin(i)

        loop(CHUNKS, work)

    @pl.when(inner & odd)
    def _():
        def begin(i):
            send(L, z, i, 0, True).start()
            send(L, z, i, 1, True).start()
            local(L, i).start()

        loop(CHUNKS, begin)
        loop(CHUNKS, lambda i: local(S, i).start())

        def both(i):
            pass_on(L, end, i)
            send(L, end, i, 0).start()

        loop(CHUNKS, both)
        loop(CHUNKS, lambda i: send(S, z, i, 1, True).start())
        for block in (z, other_mid, other_end):
            loop(CHUNKS, lambda i, block=block: wait(L, block, i))

        def across(i):
            pass_on(S, end, i)
            send(S, z, i, 0, True).start()
            send(S, end, i, 0).start()

        first_wait(1)

        def work(i):
            pass_on(R, other_mid, i)
            pass_on(R, other_end, i)
            for block in (z, end):
                wait(R, block, i)

            @pl.when(i == CHUNKS - 2)
            def _():
                loop(CHUNKS // 2, across)

            couple_and_begin(i)

        loop(CHUNKS, work)
        loop(CHUNKS, across, CHUNKS // 2)

    @pl.when(inner)
    def _():
        steps = TERMS - 1
        def advance(slot, before, after):
            tall = size // 1

            def part(t):
                r = pl.ds(pl.multiple_of(t * tall, tall), tall)
                product = jnp.dot(coupling[r, :], state[slot, before], preferred_element_type=jnp.float32)
                state[slot, after, r, :] = (first[slot, r, :].astype(jnp.float32) + product).astype(jnp.bfloat16)

            loop(1, part)

        def arrived(i):
            wait(S, z, i)

            @pl.when(even)
            def _():
                wait(S, end, i)

            @pl.when(odd)
            def _():
                for block in (other_mid, other_end):
                    wait(S, block, i)

        def far_product(i):
            arrived(i)
            far_out[rows(i), :] = jnp.dot(
                x[S, rows(i), :], state[0, steps % 2], preferred_element_type=jnp.float32
            ).astype(jnp.bfloat16)
            far(i).start()

        def near_product(i):
            result[rows(i), :] = jnp.dot(
                x[S, rows(i), :], state[1, steps % 2], preferred_element_type=jnp.float32
            )
            write(i).start()

        def relay(i):
            @pl.when(even)
            def _():
                pass_on(S, other_mid, i)
                pass_on(S, other_end, i)

        turns = steps - 1

        def early(k):
            advance(0, lax.rem(k, 2), lax.rem(k + 1, 2))

            @pl.when(lax.rem(k, 2) == 0)
            def _():
                relay(k // 2 - 1)

        def late(k):
            advance(1, lax.rem(k, 2), lax.rem(k + 1, 2))

            @pl.when(lax.rem(k, 2) == 0)
            def _():
                relay(k // 2 - 1 + turns // 2)
                far_product(k // 2 - 1 + turns // 2)

        loop(steps, early, 1)
        loop(turns // 2, far_product)
        loop(steps, late, 1)
        relay(CHUNKS - 2)
        far_product(CHUNKS - 2)
        loop(CHUNKS - 1, near_product)
        relay(CHUNKS - 1)
        far_product(CHUNKS - 1)
        near_product(CHUNKS - 1)
        loop(CHUNKS, lambda i: far(i).wait_send())
        loop(CHUNKS, lambda i: write(i).wait())

    def drain_own(m, i):
        for way in range(2):
            send(m, z, i, way, True).wait_send()
            send(m, end, i, way).wait_send()

    def drain_relay(m, i):
        send(m, other_mid, i, 1).wait_send()
        send(m, other_end, i, 1).wait_send()

    @pl.when(inner & even)
    def _():
        mate_first.wait_send()

        def drain(i):
            drain_own(R, i)
            drain_relay(L, i)
            drain_relay(S, i)

        loop(CHUNKS, drain)

    @pl.when(inner & odd)
    def _():
        def drain(i):
            drain_own(L, i)
            drain_own(S, i)
            drain_relay(R, i)

        loop(CHUNKS, drain)


def line(n, reflection, transmission):
    size, panel = reflection.shape[1:]
    width = panel // 2
    bf16 = jnp.bfloat16
    return pl.pallas_call(
        functools.partial(line_kernel, n),
        out_shape=jax.ShapeDtypeStruct((1, size, width), jnp.float32),
        in_specs=[pl.BlockSpec(memory_space=pl.ANY)] * 2,
        out_specs=pl.BlockSpec(memory_space=pl.ANY),
        scratch_shapes=[
            pltpu.VMEM((3, size, n * panel), bf16),
            pltpu.VMEM((size, n * panel), bf16),
            pltpu.VMEM((2, size, width), bf16),
            pltpu.VMEM((2, 2, size, width), bf16),
            pltpu.VMEM((size, width), bf16),
            pltpu.VMEM((size, width), bf16),
            pltpu.SemaphoreType.DMA((3, n, CHUNKS)),
            pltpu.SemaphoreType.DMA((3, n, CHUNKS, 2)),
            pltpu.SemaphoreType.DMA((2,)),
            pltpu.SemaphoreType.DMA((2,)),
            pltpu.SemaphoreType.DMA((CHUNKS,)),
            pltpu.SemaphoreType.DMA((CHUNKS,)),
            pltpu.SemaphoreType.REGULAR,
            pltpu.VMEM((size, width), jnp.float32),
            pltpu.SemaphoreType.DMA((CHUNKS,)),
        ],
        compiler_params=pltpu.CompilerParams(
            collective_id=0, has_side_effects=True, vmem_limit_bytes=60 * 2**20
        ),
    )(reflection, transmission)


def solution(mesh):
    n = mesh.shape["blk"]
    return jax.shard_map(
        functools.partial(line, n) if n == 4 else on_device,
        mesh=mesh,
        in_specs=(P(("parts", "len"), None, "blk"), P(("parts", "len"), None, "blk")),
        out_specs=P(("parts", "len"), None, "blk"),
        check_vma=False,
    )
```
